32 devices in a mesh: samp: 4 (over x, core), snp: 4 (over z), gene: 2 (over y).
Axes of the slice: x: 2, y: 2, z: 4, core: 2. Of those that a mesh axis runs over, the one named last changes fastest.
Arguments:
- dosage: bfloat16 [18432, 1024], P(('samp', 'gene'), 'snp'), may hold values from 0 to 2
- snp_scale: float32 [1024], P('snp'), may hold values from 0.5 to 2
- covariates: float32 [18432, 64], P(('samp', 'gene'))
- previous: bfloat16 [18432, 1024], P(('samp', 'gene'), 'snp')
- expression: bfloat16 [18432, 20480], P('samp', 'gene')
Outputs:
- resid: bfloat16 [18432, 1024], P(('samp', 'gene'), 'snp')
- zscores: bfloat16 [1024, 20480], P('snp', 'gene')
The draws below stay inside these ranges and needn't reach their ends.
All inputs are finite; a program needn't handle non-finite values.
Results may differ from the reference program's by a relative error of at most 0.001.
Values may be sent and summed in bfloat16 or wider, within the bound.
No kernel may reach another device: no remote copies, remote signals or barrier semaphores. Data moves between devices by JAX's collectives and lax.ppermute only.
A program may use at most 192 MiB of HBM per device.

```python
import math
import jax
import jax.numpy as jnp
from jax import lax

SNPS = 1024
GENES = 20480
COVS = 64
SAMPLES = 18432
N_GENE = 2


def sample_rise(count, top):
    position = jnp.arange(count).astype(jnp.float32)
    return 10.0 ** (top * position / count)


def shared_parts(key):
    base = jax.random.fold_in(key, 101)
    first, second, third = jax.random.split(base, 3)
    drawn = jax.random.normal(first, (SAMPLES, COVS), jnp.float32)
    mixing = jax.random.normal(second, (COVS, SNPS), jnp.float32)
    noise = jax.random.normal(third, (SAMPLES, SNPS), jnp.float32)
    return (drawn, mixing, noise)


def draw_covariates(key, part):
    drawn, mixing, noise = shared_parts(key)
    top = 0.5
    return drawn * sample_rise(SAMPLES, top)[:, None]


def draw_dosage(key, part):
    drawn, mixing, noise = shared_parts(key)
    latent = jnp.dot(drawn, mixing) / jnp.sqrt(jnp.float32(COVS))
    return (1.0 + 0.9 * jnp.tanh(0.8 * latent + 0.6 * noise)).astype(jnp.bfloat16)


def draw_previous(key, part):
    base = jax.random.fold_in(key, 202)
    first, second = jax.random.split(base, 2)
    top = 0.25
    values = jax.random.normal(first, (SAMPLES, SNPS), jnp.float32)
    column = 10.0 ** jax.random.uniform(second, (SNPS,), jnp.float32)
    return (values * sample_rise(SAMPLES, top)[:, None] * column[None, :]).astype(jnp.bfloat16)


def draw_expression(key, part):
    base = jax.random.fold_in(key, 303)
    first, second = jax.random.split(base, 2)
    values = jax.random.normal(first, (SAMPLES, GENES), jnp.float32)
    column = 10.0 ** jax.random.uniform(second, (GENES,), jnp.float32)
    top = 0.25
    return (values * sample_rise(SAMPLES, top)[:, None] * column[None, :]).astype(jnp.bfloat16)


def shard_levels(rng, shape, cuts, smallest, largest):
    level, own = 1.0, jax.random.fold_in(rng, 6)
    for axis_at, parts in cuts:
        heights = jnp.exp(jax.random.uniform(jax.random.fold_in(own, axis_at), (parts,), jnp.float32, smallest / len(cuts), largest / len(cuts)))
        level = level * jnp.repeat(heights, shape[axis_at] // parts).reshape([-1 if axis == axis_at else 1 for axis in range(len(shape))])
    return level


def setup_inputs(seed: int = 0) -> dict:
    key_list = jax.random.split(jax.random.key(seed), 6)
    dosage = draw_dosage(jax.random.fold_in(key_list[5], 71), 0)
    snp_scale = jnp.clip(jnp.exp(math.log(2.0) - 1.3862944 * jax.random.uniform(key_list[1], (SNPS,), jnp.float32) ** shard_levels(key_list[1], (SNPS,), ((0, 4),), -0.2, 0.2)), 0.5, 2.0)
    covariates = draw_covariates(jax.random.fold_in(key_list[5], 71), 0)
    previous = draw_previous(jax.random.fold_in(key_list[5], 71), 0)
    expression = draw_expression(jax.random.fold_in(key_list[5], 71), 0)
    return {"dosage": dosage, "snp_scale": snp_scale, "covariates": covariates, "previous": previous, "expression": expression}


def reference(dosage, snp_scale, covariates, previous, expression):
    highest = lax.Precision.HIGHEST
    decoded = dosage.astype(jnp.float32) * snp_scale[None, :]
    gram = jnp.dot(covariates.T, covariates, precision=highest)
    cross = jnp.dot(covariates.T, decoded, precision=highest)
    factor = jnp.linalg.cholesky(gram)
    coef = jax.scipy.linalg.cho_solve((factor, True), cross)
    resid = (decoded - jnp.dot(covariates, coef, precision=highest)).astype(jnp.bfloat16)
    genotype = previous.astype(jnp.float32)
    panels = expression.reshape(SAMPLES, N_GENE, GENES // N_GENE).transpose(1, 0, 2)

    def panel_scores(panel):
        return jnp.dot(genotype.T, panel.astype(jnp.float32), precision=highest)
    scores = lax.map(panel_scores, panels).transpose(1, 0, 2).reshape(SNPS, GENES)
    x_sq = lax.optimization_barrier(jnp.sum(genotype * genotype, axis=0))
    y_sq = jnp.einsum('sg,sg->g', expression.astype(jnp.float32), expression.astype(jnp.float32), preferred_element_type=jnp.float32)
    denom = jnp.sqrt(x_sq + 1e-06)[:, None] * jnp.sqrt(y_sq + 1e-06)[None, :]
    zscores = (jnp.sqrt(jnp.float32(SAMPLES)) * scores / denom).astype(jnp.bfloat16)
    return (resid, zscores)
```

```python
import jax
import jax.numpy as jnp
from jax import lax
from jax.experimental import pallas as pl
from jax.experimental.pallas import tpu as pltpu
from jax.sharding import PartitionSpec as P


LANES = 128
SUBLANES = 8
LAG = 3
HIGHEST = lax.Precision.HIGHEST


def swap(value, axis, bit):
    count = lax.axis_size(axis)
    return lax.ppermute(value, axis, [(i, i ^ bit) for i in range(count)])


def after(*values):
    return lax.optimization_barrier(values)


def chunk_kernel(steps, squares, start, order_ref, mine_left, early_left, late_left, right_hbm, send_ref, pass_ref, mine_ref, acc_ref, right_ref, sems):
    half, rows, depth = mine_left.shape
    width = pass_ref.shape[1]

    def fetch(step):
        part = (step // half) ^ order_ref[4]
        row = pl.multiple_of((part * half + step % half) * depth, depth)
        return pltpu.make_async_copy(
            right_hbm.at[pl.ds(row, depth), pl.ds(start, 4 * width)], right_ref.at[step], sems.at[step]
        )

    for step in range(steps):
        fetch(step).start()
    acc_ref[...] = jnp.zeros_like(acc_ref)

    @pl.loop(0, steps)
    def _(step):
        other = jnp.where(step < half + half // 2, early_left[jnp.clip(step - half, 0, half // 2 - 1)], late_left[jnp.clip(step - half - half // 2, 0, half // 2 - 1)])
        left = jnp.where(step < half, mine_left[jnp.minimum(step, half - 1)], other)
        fetch(step).wait()
        right = right_ref[step]
        acc_ref[:rows] += jnp.dot(left, right, preferred_element_type=jnp.float32)
        if squares:
            wide = right.astype(jnp.float32)
            acc_ref[rows:] += jnp.sum((wide * wide).reshape(-1, SUBLANES, 4 * width), axis=0)

    def block(at):
        return acc_ref[:, pl.ds(pl.multiple_of(order_ref[at] * width, LANES), width)]

    send_ref[0] = block(0)
    send_ref[1] = block(1)
    pass_ref[...] = block(2)
    mine_ref[...] = block(3)


def chunk_products(order, lefts, right, start, width, squares):
    half, rows, depth = lefts[0].shape
    steps = 2 * half
    high = rows + (SUBLANES if squares else 0)
    shape = jax.ShapeDtypeStruct((high, width), jnp.float32)
    vmem = pl.BlockSpec(memory_space=pltpu.VMEM)
    return pl.pallas_call(
        lambda *refs: chunk_kernel(steps, squares, start, *refs),
        out_shape=(jax.ShapeDtypeStruct((2, high, width), jnp.float32), shape, shape),
        in_specs=[pl.BlockSpec(memory_space=pltpu.SMEM), vmem, vmem, vmem, pl.BlockSpec(memory_space=pl.ANY)],
        out_specs=(vmem, vmem, vmem),
        scratch_shapes=[
            pltpu.VMEM((high, 4 * width), jnp.float32),
            pltpu.VMEM((steps, depth, 4 * width), jnp.bfloat16),
            pltpu.SemaphoreType.DMA((steps,)),
        ],
        compiler_params=pltpu.CompilerParams(vmem_limit_bytes=36 << 20),
        cost_estimate=pl.CostEstimate(flops=1000, bytes_accessed=1000, transcendentals=0),
        name="chunk_products",
    )(order, *lefts, right)


def plan(genes):
    width = 4 * LANES
    count = genes // (4 * width) - 1
    out = [(c * 4 * width, width) for c in range(count)]
    return out + [(count * 4 * width, width // 2), (count * 4 * width + 2 * width, width // 2)]


def fast(dosage, snp_scale, covariates, previous, expression):
    samp, gene = lax.axis_index("samp"), lax.axis_index("gene")
    low, high = samp & 1, samp >> 1

    def owner(h, c):
        return 2 * h + c

    order = jnp.stack([owner(1 - high, 1 - low), owner(high, 1 - low), owner(1 - high, low), owner(high, low), gene]).astype(jnp.int32)
    local, snps = previous.shape
    deep, genes = expression.shape
    samples = deep * lax.axis_size("samp")
    split = 2
    depth = local // split

    def turned(block):
        return block.reshape(-1, depth, snps).transpose(0, 2, 1)

    first_rows, previous, covariates, dosage = after(previous[:depth], previous, covariates, dosage)
    other_a = swap(first_rows, "gene", 1)

    decoded = dosage.astype(jnp.float32) * snp_scale[None, :]
    covs = covariates.shape[1]
    gram = jnp.dot(covariates.T, covariates, precision=HIGHEST)
    cross = jnp.dot(covariates.T, decoded, precision=HIGHEST)
    wide = previous.astype(jnp.float32)
    x_own = jnp.sum(wide * wide, axis=0)
    top = jnp.concatenate([cross, jnp.pad(gram, ((0, 0), (0, -covs % LANES)))], axis=1)
    bottom = jnp.pad(x_own[None], ((0, SUBLANES - 1), (0, top.shape[1] - snps)))
    sums = jnp.concatenate([top, bottom], axis=0)
    sums, last_rows = after(sums, previous[depth:])
    sums_got = swap(sums, "gene", 1)
    other_b = swap(last_rows, "gene", 1)

    for bit in (1, 2):
        sums = sums + sums_got
        sums_got = swap(sums, "samp", bit)
    sums = sums + sums_got
    order, sums = after(order, sums)
    cross, gram = sums[:covs, :snps], sums[:covs, snps : snps + covs]
    x_root = jnp.sqrt(sums[covs, :snps] + 1e-06)[:, None]
    lefts = (turned(previous), turned(other_a), turned(other_b))
    root = jnp.sqrt(jnp.float32(samples))

    zscores = jnp.zeros((snps, genes), jnp.bfloat16)
    places = (owner(high, low), owner(1 - high, low), owner(high, 1 - low), owner(1 - high, 1 - low))
    work = plan(genes)
    onwards, z_owns, pending = [], [], []
    for at in range(len(work) + LAG):
        if at < len(work):
            start, width = work[at]
            if at >= 2:
                order, onwards[at - 2] = after(order, onwards[at - 2])
            if at >= LAG:
                order, z_owns[at - LAG] = after(order, z_owns[at - LAG])
            send, onward, mine = chunk_products(order, lefts, expression, start, width, True)
            got = swap(send, "samp", 1)
            onwards.append(onward + got[0])
            pending.append((mine, got))
        back = at - LAG + 1
        if 0 <= back < len(work):
            mine, got = pending[back]
            far = swap(onwards[back], "samp", 2)
            x_root, far = after(x_root, far)
            share = mine + got[1] + far
            y_root = jnp.sqrt(jnp.sum(share[snps:], axis=0) + 1e-06)[None, :]
            z_owns.append((root * share[:snps] / (x_root * y_root)).astype(jnp.bfloat16))
    gram, cross, onwards[-1] = after(gram, cross, onwards[-1])
    factor = jnp.linalg.cholesky(gram)
    coef = jax.scipy.linalg.cho_solve((factor, True), cross)
    resid = (decoded - jnp.dot(covariates, coef, precision=HIGHEST)).astype(jnp.bfloat16)
    resid, z_owns[-2] = after(resid, z_owns[-2])
    for at, (start, width) in enumerate(work):
        z_own = z_owns[at]
        z_far = swap(z_own, "samp", 2)
        pieces = (z_own, z_far, swap(z_own, "samp", 1), swap(z_far, "samp", 1))
        block = []
        for spot in range(4):
            value = pieces[3]
            for near in range(3):
                value = jnp.where(places[near] == spot, pieces[near], value)
            block.append(value)
        zscores = lax.dynamic_update_slice(zscores, jnp.concatenate(block, axis=1), (0, start))

    return (resid, zscores)


def general(dosage, snp_scale, covariates, previous, expression):
    decoded = dosage.astype(jnp.float32) * snp_scale[None, :]
    gram = jnp.dot(covariates.T, covariates, precision=HIGHEST)
    cross = jnp.dot(covariates.T, decoded, precision=HIGHEST)
    gram, cross = lax.psum((gram, cross), ("samp", "gene"))
    factor = jnp.linalg.cholesky(gram)
    coef = jax.scipy.linalg.cho_solve((factor, True), cross)
    resid = (decoded - jnp.dot(covariates, coef, precision=HIGHEST)).astype(jnp.bfloat16)
    piece = lax.all_gather(previous, "gene", axis=0, tiled=True)
    partial = lax.dot_general(
        piece, expression, (((0,), (0,)), ((), ())), preferred_element_type=jnp.float32
    )
    x_sq = jnp.einsum("sp,sp->p", piece, piece, preferred_element_type=jnp.float32)
    y_sq = jnp.einsum("sg,sg->g", expression, expression, preferred_element_type=jnp.float32)
    samples = expression.shape[0] * lax.axis_size("samp")
    root = jnp.sqrt(jnp.float32(samples))
    shares = lax.psum_scatter(partial, "samp", scatter_dimension=1, tiled=True)
    y_share = lax.psum_scatter(y_sq, "samp", scatter_dimension=0, tiled=True)
    x_sq = lax.psum(x_sq, "samp")
    denom = jnp.sqrt(x_sq + 1e-06)[:, None] * jnp.sqrt(y_share + 1e-06)[None, :]
    z_part = (root * shares / denom).astype(jnp.bfloat16)
    return (resid, lax.all_gather(z_part, "samp", axis=1, tiled=True))


def solution(mesh):
    placed = (
        P(("samp", "gene"), "snp"),
        P("snp"),
        P(("samp", "gene"), None),
        P(("samp", "gene"), "snp"),
        P("samp", "gene"),
    )

    def on_device(*args):
        genes, snps = args[4].shape[1], args[3].shape[1]
        fits = mesh.shape["samp"] == 4 and mesh.shape["gene"] == 2
        fits = fits and genes % (16 * LANES) == 0 and genes >= 48 * LANES and snps % LANES == 0 and args[3].shape[0] % (2 * LANES) == 0
        return fast(*args) if fits else general(*args)

    return jax.shard_map(
        on_device,
        mesh=mesh,
        in_specs=placed,
        out_specs=(P(("samp", "gene"), "snp"), P("snp", "gene")),
        check_vma=False,
    )
```
